32 devices in a mesh: mem: 4 (over y, x), tile: 8 (over z, core).
Axes of the slice: x: 2, y: 2, z: 4, core: 2. Of those that a mesh axis runs over, the one named last changes fastest.
Arguments:
- perturbations: bfloat16 [96, 3, 32, 8192], P('mem', None, None, 'tile'), may hold values from -6 to 6
- member_weight: float32 [96], P('mem'), may hold values from 0.3 to 3
- innovation: float32 [3, 32, 8192], P(None, 'mem', 'tile'), may hold values from -6 to 6
- obs_weight: float32 [3, 32], P(None, 'mem'), may hold values from 0.1 to 1
- static_var: float32 [3, 32, 8192], P(None, 'mem', 'tile'), may hold values from 0.1 to 1
- obs_mask: int32 [8192], P('tile'), may hold values 0 or 1
- kernel_x: float32 [32, 5], replicated, may hold values from 0.1 to 0.5
- kernel_y: float32 [32, 5], replicated, may hold values from 0.1 to 0.5
Outputs:
- analysis: float32 [3, 32, 8192], P(None, 'mem', 'tile')
The draws below stay inside these ranges and needn't reach their ends.
All inputs are finite; a program needn't handle non-finite values. No bound on the sum of `obs_mask` on one device may be relied on, other than what follows from the above.
Results may differ from the reference program's by a relative error of at most 0.0003.
Values sent between devices are 32-bit elements; how exact they have to be, the bound alone decides.
A program may use at most 64 MiB of HBM per device.

```python
import math
import jax
import jax.numpy as jnp
from jax import lax

VARS = 3
LEVELS = 32
TILE_X = 32
TILE_Y = 32
GRID_Y = 4
STEPS = 2
MEMBER_COUNT_NUM = 96
NCOL = 8192
N_MEM = 4
N_TILE = 8


def touch_ends(result, own_key, smallest, top_value):
    place = [jax.random.randint(jax.random.fold_in(own_key, axis), (), 0, length) for axis, length in enumerate(result.shape)]
    main_axis = result.shape.index(max(result.shape))
    neighbour = place[:main_axis] + [(place[main_axis] + 1) % result.shape[main_axis]] + place[main_axis + 1:]
    return result.at[tuple(place)].set(smallest).at[tuple(neighbour)].set(top_value)


def levels(key, extent, shards, least, largest):
    factor_of, own = 1.0, jax.random.fold_in(key, 6)
    for dim, blocks in shards:
        steps = jnp.exp(jax.random.uniform(jax.random.fold_in(own, dim), (blocks,), jnp.float32, least / len(shards), largest / len(shards)))
        factor_of = factor_of * jnp.repeat(steps, extent[dim] // blocks).reshape([-1 if axis == dim else 1 for axis in range(len(extent))])
    return factor_of


def noise(key, extent, scale, most, pieces=(), kind=jnp.bfloat16):
    loudness = levels(key, extent, pieces, -0.22, 0.18) if pieces else 1.0
    drawn = jax.random.normal(key, extent, jnp.float32) * scale * loudness
    return jnp.minimum(jnp.maximum(drawn, -most), most).astype(kind)


def setup_inputs(seed: int = 0) -> dict:
    key_list = jax.random.split(jax.random.key(seed), 9)
    perturbations = noise(key_list[0], (MEMBER_COUNT_NUM, VARS, LEVELS, NCOL), 1.0, 6.0, ((0, 4), (3, 8)))
    member_weight = jnp.clip(jnp.exp(math.log(3.0) - 2.3025851 * jax.random.uniform(key_list[1], (MEMBER_COUNT_NUM,), jnp.float32) ** levels(key_list[1], (MEMBER_COUNT_NUM,), ((0, 4),), -0.2, 0.2)), 0.3, 3.0)
    innovation = noise(key_list[2], (VARS, LEVELS, NCOL), 1.0, 6.0, ((1, 4), (2, 8)), jnp.float32)
    obs_weight = jnp.clip(jnp.exp(math.log(1.0) - 2.3025851 * jax.random.uniform(key_list[3], (VARS, LEVELS), jnp.float32) ** levels(key_list[3], (VARS, LEVELS), ((1, 4),), -0.2, 0.2)), 0.1, 1.0)
    static_var = jnp.clip(jnp.exp(math.log(1.0) - 2.3025851 * jax.random.uniform(key_list[4], (VARS, LEVELS, NCOL), jnp.float32) ** levels(key_list[4], (VARS, LEVELS, NCOL), ((1, 4), (2, 8)), -0.2, 0.2)), 0.1, 1.0)
    obs_mask = touch_ends((jax.random.randint(key_list[5], (NCOL,), 0, 2) < 1).astype(jnp.int32), jax.random.fold_in(key_list[5], 1), 0, 1)
    kernel_x = jnp.clip(jnp.exp(jax.random.uniform(key_list[6], (LEVELS, 5), jnp.float32, math.log(0.1), math.log(0.5))), 0.1, 0.5)
    kernel_y = jnp.clip(jnp.exp(jax.random.uniform(key_list[7], (LEVELS, 5), jnp.float32, math.log(0.1), math.log(0.5))), 0.1, 0.5)
    return dict(perturbations=perturbations, member_weight=member_weight, innovation=innovation, obs_weight=obs_weight, static_var=static_var, obs_mask=obs_mask, kernel_x=kernel_x, kernel_y=kernel_y)


def interp_rows(fine_count, coarse_count):
    position = jnp.arange(fine_count, dtype=jnp.int32)
    lower_index = jnp.clip((position - 1) // 2, 0, coarse_count - 1)
    upper_index = jnp.clip((position - 1) // 2 + 1, 0, coarse_count - 1)
    fraction = jnp.where(position % 2 == 0, 0.75, 0.25).astype(jnp.float32)
    columns = jnp.arange(coarse_count, dtype=jnp.int32)
    lower_part = (lower_index[:, None] == columns[None, :]).astype(jnp.float32)
    upper_part = (upper_index[:, None] == columns[None, :]).astype(jnp.float32)
    return (1.0 - fraction)[:, None] * lower_part + fraction[:, None] * upper_part


def localize_all(member_projection, kernel_x, kernel_y, rows_x, rows_y):
    members = member_projection.shape[0]
    coarse_x = TILE_X // 2
    coarse_y = TILE_Y // 2
    grid_x = N_TILE // GRID_Y
    tiled = member_projection.reshape(members, LEVELS, N_TILE, TILE_X, TILE_Y)
    half = jnp.einsum("mltij,ia->mltaj", tiled, rows_x, precision=lax.Precision.HIGHEST)
    coarse = jnp.einsum("mltaj,jb->mltab", half, rows_y, precision=lax.Precision.HIGHEST)
    coarse = coarse.reshape(members, LEVELS, grid_x, GRID_Y, coarse_x, coarse_y)
    coarse = coarse.transpose(0, 1, 2, 4, 3, 5).reshape(members, LEVELS, grid_x * coarse_x, GRID_Y * coarse_y)
    summed_x = jnp.zeros_like(coarse)
    for offset in range(5):
        summed_x = summed_x + kernel_x[:, offset][None, :, None, None] * jnp.roll(coarse, 2 - offset, axis=2)
    padded = jnp.pad(summed_x, ((0, 0), (0, 0), (0, 0), (2, 2)))
    extent_y = GRID_Y * coarse_y
    summed_y = jnp.zeros_like(coarse)
    for offset in range(5):
        summed_y = summed_y + kernel_y[:, offset][None, :, None, None] * padded[:, :, :, offset:offset + extent_y]
    smoothed = summed_y.reshape(members, LEVELS, grid_x, coarse_x, GRID_Y, coarse_y)
    smoothed = smoothed.transpose(0, 1, 2, 4, 3, 5).reshape(members, LEVELS, N_TILE, coarse_x, coarse_y)
    half_fine = jnp.einsum("mltab,ia->mltib", smoothed, rows_x, precision=lax.Precision.HIGHEST)
    fine_resolution_state = jnp.einsum("mltib,jb->mltij", half_fine, rows_y, precision=lax.Precision.HIGHEST)
    return fine_resolution_state.reshape(members, LEVELS, NCOL)


def reference(perturbations, member_weight, innovation, obs_weight, static_var, obs_mask, kernel_x, kernel_y):
    rows_x = interp_rows(TILE_X, TILE_X // 2)
    rows_y = interp_rows(TILE_Y, TILE_Y // 2)
    observed = obs_mask.astype(jnp.float32)
    within_each_tile = MEMBER_COUNT_NUM // N_MEM
    blocks = perturbations.reshape(N_MEM, within_each_tile, VARS, LEVELS, NCOL)
    weight_blocks = member_weight.reshape(N_MEM, within_each_tile)

    def apply_ensemble(cost_gradient):
        def accumulate(summed, scanned):
            member_block, analysis_coefficients = scanned
            multi_tile_extent = member_block.astype(jnp.float32)
            member_projection = jnp.einsum("ohjr,hjr->ojr", multi_tile_extent, cost_gradient, precision=lax.Precision.HIGHEST)
            fine_resolution_state = localize_all(member_projection, kernel_x, kernel_y, rows_x, rows_y)
            addend_contribution = jnp.einsum("v,vhyp,vyp->hyp", analysis_coefficients / MEMBER_COUNT_NUM, multi_tile_extent, fine_resolution_state, precision=lax.Precision.HIGHEST)
            return summed + addend_contribution, None

        start = jnp.zeros((VARS, LEVELS, NCOL), jnp.float32)
        summed, _ = lax.scan(accumulate, start, (blocks, weight_blocks))
        return summed

    analysis = jnp.zeros((VARS, LEVELS, NCOL), jnp.float32)
    for repeat in range(STEPS):
        cost_gradient = observed[None, None, :] * obs_weight[:, :, None] * (analysis - innovation)
        increment = apply_ensemble(cost_gradient) + static_var * cost_gradient
        analysis = analysis - 0.5 * (analysis + increment)
    return analysis
```

```python
import functools

import jax
import jax.numpy as jnp
import numpy as np
from jax import lax
from jax.experimental import pallas as pl
from jax.experimental.pallas import tpu as pltpu
from jax.sharding import PartitionSpec as P

TILE_X = 32
TILE_Y = 32
GRID_Y = 4
STEPS = 2
COARSE_X = TILE_X // 2
COARSE_Y = TILE_Y // 2
COARSE = COARSE_X * COARSE_Y
GROUP_LEVELS = 16
LANES = 256
MESH = pl.DeviceIdType.MESH
F32 = jnp.float32
BF16 = jnp.bfloat16


def interp_rows(fine_count):
    coarse_count = fine_count // 2
    rows = np.zeros((fine_count, coarse_count), np.float32)
    for i in range(fine_count):
        low = min(max((i - 1) // 2, 0), coarse_count - 1)
        high = min(max((i - 1) // 2 + 1, 0), coarse_count - 1)
        fraction = 0.75 if i % 2 == 0 else 0.25
        rows[i, low] += 1.0 - fraction
        rows[i, high] += fraction
    return rows


def interp_matrix():
    rows_x, rows_y = interp_rows(TILE_X), interp_rows(TILE_Y)
    whole = rows_x[:, None, None, :] * rows_y[None, :, :, None]
    return whole.reshape(TILE_X * TILE_Y, COARSE)


def rolled(x, by):
    by = by % x.shape[1]
    return x if by == 0 else pltpu.roll(x, by, 1)


def split(x):
    high = x.astype(BF16)
    return high, (x - high.astype(F32)).astype(BF16)


def kernel(
    n_mem, n_tile,
    pert_hbm, weight_ref, innov_ref, obsw_ref, static_ref, mask_ref, kx_ref, ky_ref, down_ref, up_ref,
    out_ref,
    pert, obs, ana, gbuf, part, rsbuf, gfull, alpha_hi, alpha_lo, coarse, smooth, fine,
    kxb, kyb, sendbuf, halo,
    pert_sem, ag_send, ag_recv, rs_send, rs_recv, halo_send, halo_recv,
):
    members, nvar, levels, cols = pert.shape
    own_levels = innov_ref.shape[1]
    n_group = levels // GROUP_LEVELS
    owners = GROUP_LEVELS // own_levels
    rows = members * GROUP_LEVELS
    packs = COARSE_X // 2
    prow = rows // packs
    grid_x = n_tile // GRID_Y
    me = lax.axis_index("mem")
    tile = lax.axis_index("tile")
    place_y = lax.rem(tile, GRID_Y)
    next_x = lax.rem(tile + GRID_Y, n_tile)
    prev_x = lax.rem(tile + n_tile - GRID_Y, n_tile)
    has_prev = place_y > 0
    has_next = place_y < GRID_Y - 1

    load = pltpu.make_async_copy(pert_hbm, pert, pert_sem)
    load.start()

    barrier = pltpu.get_barrier_semaphore()

    def greet(device_id):
        pl.semaphore_signal(barrier, inc=1, device_id=device_id, device_id_type=MESH)

    for i in range(1, n_mem):
        greet((lax.rem(me + i, n_mem), tile))
    greet((me, next_x))
    if grid_x > 2:
        greet((me, prev_x))

    greet((me, tile - place_y + lax.rem(place_y + GRID_Y - 1, GRID_Y)))
    greet((me, tile - place_y + lax.rem(place_y + 1, GRID_Y)))

    mask = mask_ref[...].astype(F32)
    for v in range(nvar):
        for l in range(own_levels):
            obs[v, l : l + 1, :] = mask * obsw_ref[v, l]
    ana[...] = jnp.zeros_like(ana)
    gbuf[0, me] = obs[...] * (ana[...] - innov_ref[...])

    pl.semaphore_wait(barrier, n_mem - 1 + min(grid_x - 1, 2) + 2)

    def gather_to(step, i):
        return pltpu.make_async_remote_copy(
            src_ref=gbuf.at[step, me], dst_ref=gbuf.at[step, me],
            send_sem=ag_send.at[step, i], recv_sem=ag_recv.at[step, me],
            device_id=(lax.rem(me + i, n_mem), tile), device_id_type=MESH,
        )

    def gathered_from(step, owner):
        return pltpu.make_async_remote_copy(
            src_ref=gbuf.at[step, owner], dst_ref=gbuf.at[step, owner],
            send_sem=ag_send.at[step, 0], recv_sem=ag_recv.at[step, owner],
            device_id=(owner, tile), device_id_type=MESH,
        )

    def reduce_to(step, owner):
        return pltpu.make_async_remote_copy(
            src_ref=part.at[step, owner], dst_ref=rsbuf.at[step, me],
            send_sem=rs_send.at[step, owner], recv_sem=rs_recv.at[step, me],
            device_id=(owner, tile), device_id_type=MESH,
        )

    def reduced_from(step, source):
        return pltpu.make_async_remote_copy(
            src_ref=part.at[step, source], dst_ref=rsbuf.at[step, source],
            send_sem=rs_send.at[step, source], recv_sem=rs_recv.at[step, source],
            device_id=(source, tile), device_id_type=MESH,
        )

    def halo_copy(step, group, way, side):
        target = ((tile + 1, tile - 1), (next_x, prev_x))[way][side]
        return pltpu.make_async_remote_copy(
            src_ref=sendbuf.at[step, group, way, side], dst_ref=halo.at[step, group, way, side],
            send_sem=halo_send.at[step, group, way, side],
            recv_sem=halo_recv.at[step, group, way, side],
            device_id=(me, target), device_id_type=MESH,
        )

    for i in range(1, n_mem):
        gather_to(0, i).start()

    for d in range(5):
        kxb[d] = jnp.broadcast_to(kx_ref[:, d : d + 1], (levels, COARSE))
        kyb[d] = jnp.broadcast_to(ky_ref[:, d : d + 1], (levels, COARSE))

    @pl.when(jnp.logical_not(has_prev))
    def _():
        for step in range(STEPS):
            for group in range(n_group):
                halo[step, group, 0, 0] = jnp.zeros((prow, COARSE), F32)

    @pl.when(jnp.logical_not(has_next))
    def _():
        for step in range(STEPS):
            for group in range(n_group):
                halo[step, group, 0, 1] = jnp.zeros((prow, COARSE), F32)

    lane = lax.broadcasted_iota(jnp.int32, (prow, COARSE), 1)
    index = (lane // COARSE_X, lane % COARSE_X)
    stride = (COARSE_X, 1)

    def pack(step, group, way):
        slot = index[way] // 2
        unit = 2 * stride[way]
        for side, source in ((0, (packs * 2 - 2) * stride[way]), (1, 0)):
            packed = None
            for q in range(packs):
                piece = coarse[group, q * prow : (q + 1) * prow, :]
                piece = rolled(piece, unit * q - source)
                packed = piece if packed is None else jnp.where(slot == q, piece, packed)
            sendbuf[step, group, way, side] = packed

    def convolve(step, group, way, q, weights):
        at, by = index[way], stride[way]
        count = packs * 2
        x = coarse[group, q * prow : (q + 1) * prow, :]
        before = rolled(halo[step, group, way, 0], -2 * by * q)
        after = rolled(halo[step, group, way, 1], (count - 2) * by - 2 * by * q)
        taps = (
            jnp.where(at < 2, before, rolled(x, 2 * by)),
            jnp.where(at < 1, rolled(before, -by), rolled(x, by)),
            x,
            jnp.where(at >= count - 1, rolled(after, by), rolled(x, -by)),
            jnp.where(at >= count - 2, after, rolled(x, -2 * by)),
        )
        total = None
        for d in range(5):
            k = weights[d, group * GROUP_LEVELS : (group + 1) * GROUP_LEVELS, :]
            k = jnp.concatenate([k] * (prow // GROUP_LEVELS), axis=0)
            total = k * taps[d] if total is None else total + k * taps[d]
        return total

    def project(step, group):
        for o in range(owners):
            owner = group * owners + o

            @pl.when(owner != me)
            def _():
                gathered_from(step, owner).wait_recv()

            for v in range(nvar):
                gfull[v, o * own_levels : (o + 1) * own_levels, :] = gbuf[step, owner, v]

        def one(j, carry):
            at = pl.ds(pl.multiple_of(j * LANES, LANES), LANES)
            g = [gfull[v, :, at] for v in range(nvar)]
            for k in range(members):
                total = None
                for v in range(nvar):
                    term = pert[k, v, group * GROUP_LEVELS : (group + 1) * GROUP_LEVELS, at].astype(F32) * g[v]
                    total = term if total is None else total + term
                high, low = split(total)
                alpha_hi[k * GROUP_LEVELS : (k + 1) * GROUP_LEVELS, at] = high
                alpha_lo[k * GROUP_LEVELS : (k + 1) * GROUP_LEVELS, at] = low
            return carry

        lax.fori_loop(0, cols // LANES, one, 0)
        coarse[group] = jnp.dot(
            alpha_hi[...], down_ref[...], preferred_element_type=F32
        ) + jnp.dot(alpha_lo[...], down_ref[...], preferred_element_type=F32)
        pack(step, group, 0)

        @pl.when(has_next)
        def _():
            halo_copy(step, group, 0, 0).start()

        @pl.when(has_prev)
        def _():
            halo_copy(step, group, 0, 1).start()

    def smooth_y(step, group):
        @pl.when(has_prev)
        def _():
            halo_copy(step, group, 0, 0).wait_recv()

        @pl.when(has_next)
        def _():
            halo_copy(step, group, 0, 1).wait_recv()

        for q in range(packs):
            done = convolve(step, group, 0, q, kyb)
            coarse[group, q * prow : (q + 1) * prow, :] = done
        pack(step, group, 1)
        halo_copy(step, group, 1, 0).start()
        halo_copy(step, group, 1, 1).start()

    def expand(step, group):
        halo_copy(step, group, 1, 0).wait_recv()
        halo_copy(step, group, 1, 1).wait_recv()
        each = prow // GROUP_LEVELS
        for q in range(packs):
            done = convolve(step, group, 1, q, kxb)
            factor = jnp.concatenate(
                [
                    jnp.full((GROUP_LEVELS, COARSE), weight_ref[q * each + m] * (1.0 / (n_mem * members)), F32)
                    for m in range(each)
                ],
                axis=0,
            )
            high, low = split(done * factor)
            smooth[q * prow : (q + 1) * prow, :COARSE] = high
            smooth[q * prow : (q + 1) * prow, COARSE:] = low
        fine[...] = jnp.dot(smooth[...], up_ref[...], preferred_element_type=F32)

        def one(j, carry):
            at = pl.ds(pl.multiple_of(j * LANES, LANES), LANES)
            total = [None] * nvar
            for k in range(members):
                f = fine[k * GROUP_LEVELS : (k + 1) * GROUP_LEVELS, at]
                for v in range(nvar):
                    term = pert[k, v, group * GROUP_LEVELS : (group + 1) * GROUP_LEVELS, at].astype(F32) * f
                    total[v] = term if total[v] is None else total[v] + term
            for o in range(owners):
                for v in range(nvar):
                    part[step, group * owners + o, v, :, at] = total[v][o * own_levels : (o + 1) * own_levels]
            return carry

        lax.fori_loop(0, cols // LANES, one, 0)
        for o in range(owners):
            owner = group * owners + o

            @pl.when(owner != me)
            def _():
                reduce_to(step, owner).start()

    def update(step, group):
        @pl.when(me // owners == group)
        def _():
            total = static_ref[...] * gbuf[step, me] + part[step, me]
            for i in range(1, n_mem):
                source = lax.rem(me + i, n_mem)
                reduced_from(step, source).wait_recv()
                total = total + rsbuf[step, source]
            now = ana[...]
            now = now - 0.5 * (now + total)
            if step == STEPS - 1:
                out_ref[...] = now
            else:
                ana[...] = now
                gbuf[step + 1, me] = obs[...] * (now - innov_ref[...])
                for i in range(1, n_mem):
                    gather_to(step + 1, i).start()

    load.wait()
    for step in range(STEPS):
        for stage in (project, smooth_y, expand, update):
            for group in range(n_group):
                stage(step, group)

    for step in range(STEPS):
        for i in range(1, n_mem):
            gather_to(step, i).wait_send()
        for owner in range(n_mem):

            @pl.when(owner != me)
            def _():
                reduce_to(step, owner).wait_send()

        for group in range(n_group):

            @pl.when(has_next)
            def _():
                halo_copy(step, group, 0, 0).wait_send()

            @pl.when(has_prev)
            def _():
                halo_copy(step, group, 0, 1).wait_send()

            halo_copy(step, group, 1, 0).wait_send()
            halo_copy(step, group, 1, 1).wait_send()


def body(n_mem, n_tile, perturbations, member_weight, innovation, obs_weight, static_var, obs_mask, kernel_x, kernel_y):
    members, nvar, levels, cols = perturbations.shape
    own = innovation.shape[1]
    n_group = levels // GROUP_LEVELS
    rows = members * GROUP_LEVELS
    prow = rows // (COARSE_X // 2)
    down = interp_matrix()
    down_b = jnp.asarray(down, BF16)
    up_b = jnp.asarray(np.concatenate([down.T, down.T], axis=0), BF16)
    vmem = pl.BlockSpec(memory_space=pltpu.VMEM)
    smem = pl.BlockSpec(memory_space=pltpu.SMEM)
    dma = pltpu.SemaphoreType.DMA
    return pl.pallas_call(
        functools.partial(kernel, n_mem, n_tile),
        out_shape=jax.ShapeDtypeStruct(innovation.shape, F32),
        in_specs=[pl.BlockSpec(memory_space=pl.ANY), smem, vmem, smem, vmem, vmem, vmem, vmem, vmem, vmem],
        out_specs=vmem,
        scratch_shapes=[
            pltpu.VMEM(perturbations.shape, BF16),
            pltpu.VMEM(innovation.shape, F32),
            pltpu.VMEM(innovation.shape, F32),
            pltpu.VMEM((STEPS, n_mem) + innovation.shape, F32),
            pltpu.VMEM((STEPS, n_mem) + innovation.shape, F32),
            pltpu.VMEM((STEPS, n_mem) + innovation.shape, F32),
            pltpu.VMEM((nvar, GROUP_LEVELS, cols), F32),
            pltpu.VMEM((rows, cols), BF16),
            pltpu.VMEM((rows, cols), BF16),
            pltpu.VMEM((n_group, rows, COARSE), F32),
            pltpu.VMEM((rows, 2 * COARSE), BF16),
            pltpu.VMEM((rows, cols), F32),
            pltpu.VMEM((5, levels, COARSE), F32),
            pltpu.VMEM((5, levels, COARSE), F32),
            pltpu.VMEM((STEPS, n_group, 2, 2, prow, COARSE), F32),
            pltpu.VMEM((STEPS, n_group, 2, 2, prow, COARSE), F32),
            dma,
            dma((STEPS, n_mem)),
            dma((STEPS, n_mem)),
            dma((STEPS, n_mem)),
            dma((STEPS, n_mem)),
            dma((STEPS, n_group, 2, 2)),
            dma((STEPS, n_group, 2, 2)),
        ],
        compiler_params=pltpu.CompilerParams(
            collective_id=0, has_side_effects=True, vmem_limit_bytes=48 * 1024 * 1024
        ),
    )(
        perturbations, member_weight, innovation, obs_weight, static_var,
        obs_mask.reshape(1, cols), kernel_x, kernel_y, down_b, up_b,
    )


def solution(mesh):
    placed = (
        P("mem", None, None, "tile"),
        P("mem"),
        P(None, "mem", "tile"),
        P(None, "mem"),
        P(None, "mem", "tile"),
        P("tile"),
        P(),
        P(),
    )
    return jax.shard_map(
        functools.partial(body, mesh.shape["mem"], mesh.shape["tile"]),
        mesh=mesh, in_specs=placed, out_specs=P(None, "mem", "tile"), check_vma=False,
    )
```

```python
import functools

import jax
import jax.numpy as jnp
import numpy as np
from jax import lax
from jax.experimental import pallas as pl
from jax.experimental.pallas import tpu as pltpu
from jax.sharding import PartitionSpec as P

TILE_X = 32
TILE_Y = 32
GRID_Y = 4
STEPS = 2
COARSE_X = TILE_X // 2
COARSE_Y = TILE_Y // 2
COARSE = COARSE_X * COARSE_Y
GROUP_LEVELS = 8
DUE = (0.0, 2.4, 5.0, 11.0)
PERIOD = 17.0
PACE = 2.1
LANES = 256
MESH = pl.DeviceIdType.MESH
F32 = jnp.float32
BF16 = jnp.bfloat16


def interp_rows(fine_count):
    coarse_count = fine_count // 2
    rows = np.zeros((fine_count, coarse_count), np.float32)
    for i in range(fine_count):
        low = min(max((i - 1) // 2, 0), coarse_count - 1)
        high = min(max((i - 1) // 2 + 1, 0), coarse_count - 1)
        fraction = 0.75 if i % 2 == 0 else 0.25
        rows[i, low] += 1.0 - fraction
        rows[i, high] += fraction
    return rows


def interp_matrix():
    rows_x, rows_y = interp_rows(TILE_X), interp_rows(TILE_Y)
    whole = rows_x[:, None, None, :] * rows_y[None, :, :, None]
    return whole.reshape(TILE_X * TILE_Y, COARSE)


def rolled(x, by):
    by = by % x.shape[1]
    return x if by == 0 else pltpu.roll(x, by, 1)


def split(x):
    high = x.astype(BF16)
    return high, (x - high.astype(F32)).astype(BF16)


def kernel(
    n_mem, n_tile,
    pert_hbm, weight_hbm, innov_hbm, obsw_hbm, static_hbm, mask_hbm, kx_hbm, ky_hbm, down_hbm, up_hbm,
    out_ref,
    weight_ref, innov_ref, obsw_ref, static_ref, mask_ref, kx_ref, ky_ref, down_ref, up_ref,
    pert, obs, ana, gbuf, part, rsbuf, gfull, alpha_hi, alpha_lo, coarse, smooth, fine,
    kxb, kyb, sendbuf, halo,
    load_sem, ag_send, ag_recv, rs_send, rs_recv, halo_send, halo_recv,
):
    members, nvar, levels, cols = pert.shape
    own_levels = innov_ref.shape[1]
    n_group = levels // GROUP_LEVELS
    owners = GROUP_LEVELS // own_levels
    rows = members * GROUP_LEVELS
    packs = COARSE_X // 2
    prow = rows // packs
    grid_x = n_tile // GRID_Y
    me = lax.axis_index("mem")
    tile = lax.axis_index("tile")
    place_y = lax.rem(tile, GRID_Y)
    next_x = lax.rem(tile + GRID_Y, n_tile)
    prev_x = lax.rem(tile + n_tile - GRID_Y, n_tile)
    has_prev = place_y > 0
    has_next = place_y < GRID_Y - 1

    pairs = (
        (innov_hbm, innov_ref), (mask_hbm, mask_ref), (obsw_hbm, obsw_ref),
        (kx_hbm, kx_ref), (ky_hbm, ky_ref), (pert_hbm, pert), (down_hbm, down_ref),
        (weight_hbm, weight_ref), (static_hbm, static_ref), (up_hbm, up_ref),
    )
    loads = [pltpu.make_async_copy(a, b, load_sem.at[i]) for i, (a, b) in enumerate(pairs)]
    for load in loads:
        load.start()

    barrier = pltpu.get_barrier_semaphore()

    def greet(device_id):
        pl.semaphore_signal(barrier, inc=1, device_id=device_id, device_id_type=MESH)

    for i in range(1, n_mem):
        greet((lax.rem(me + i, n_mem), tile))
    greet((me, next_x))
    if grid_x > 2:
        greet((me, prev_x))

    greet((me, tile - place_y + lax.rem(place_y + GRID_Y - 1, GRID_Y)))
    greet((me, tile - place_y + lax.rem(place_y + 1, GRID_Y)))

    for load in loads[:3]:
        load.wait()
    mask = mask_ref[...].astype(F32)
    for v in range(nvar):
        for l in range(own_levels):
            obs[v, l : l + 1, :] = mask * obsw_ref[v, l]
    ana[...] = jnp.zeros_like(ana)
    gbuf[0, me] = obs[...] * (ana[...] - innov_ref[...])

    pl.semaphore_wait(barrier, n_mem - 1 + min(grid_x - 1, 2) + 2)

    def gather_to(step, i):
        return pltpu.make_async_remote_copy(
            src_ref=gbuf.at[step, me], dst_ref=gbuf.at[step, me],
            send_sem=ag_send.at[step, i], recv_sem=ag_recv.at[step, me],
            device_id=(lax.rem(me + i, n_mem), tile), device_id_type=MESH,
        )

    def gathered_from(step, owner):
        return pltpu.make_async_remote_copy(
            src_ref=gbuf.at[step, owner], dst_ref=gbuf.at[step, owner],
            send_sem=ag_send.at[step, 0], recv_sem=ag_recv.at[step, owner],
            device_id=(owner, tile), device_id_type=MESH,
        )

    def reduce_to(step, owner):
        return pltpu.make_async_remote_copy(
            src_ref=part.at[step, owner], dst_ref=rsbuf.at[step, me],
            send_sem=rs_send.at[step, owner], recv_sem=rs_recv.at[step, me],
            device_id=(owner, tile), device_id_type=MESH,
        )

    def reduced_from(step, source):
        return pltpu.make_async_remote_copy(
            src_ref=part.at[step, source], dst_ref=rsbuf.at[step, source],
            send_sem=rs_send.at[step, source], recv_sem=rs_recv.at[step, source],
            device_id=(source, tile), device_id_type=MESH,
        )

    def halo_copy(step, group, way, side):
        target = ((tile + 1, tile - 1), (next_x, prev_x))[way][side]
        return pltpu.make_async_remote_copy(
            src_ref=sendbuf.at[step, group, way, side], dst_ref=halo.at[step, group, way, side],
            send_sem=halo_send.at[step, group, way, side],
            recv_sem=halo_recv.at[step, group, way, side],
            device_id=(me, target), device_id_type=MESH,
        )

    for i in range(1, n_mem):
        gather_to(0, i).start()

    for load in loads[3:5]:
        load.wait()
    shape = (levels, levels)
    diagonal = lax.broadcasted_iota(jnp.int32, shape, 0) == lax.broadcasted_iota(jnp.int32, shape, 1)
    for source, spread in ((kx_ref, kxb), (ky_ref, kyb)):
        for d in range(5):
            column = jnp.where(diagonal, jnp.broadcast_to(source[d : d + 1, :], shape), 0.0)
            spread[d] = jnp.broadcast_to(jnp.sum(column, axis=1, keepdims=True), (levels, COARSE))

    @pl.when(jnp.logical_not(has_prev))
    def _():
        for step in range(STEPS):
            for group in range(n_group):
                halo[step, group, 0, 0] = jnp.zeros((prow, COARSE), F32)

    @pl.when(jnp.logical_not(has_next))
    def _():
        for step in range(STEPS):
            for group in range(n_group):
                halo[step, group, 0, 1] = jnp.zeros((prow, COARSE), F32)

    lane = lax.broadcasted_iota(jnp.int32, (prow, COARSE), 1)
    index = (lane // COARSE_X, lane % COARSE_X)
    stride = (COARSE_X, 1)

    def pack(step, group, way):
        slot = index[way] // 2
        unit = 2 * stride[way]
        for side, source in ((0, (packs * 2 - 2) * stride[way]), (1, 0)):
            packed = None
            for q in range(packs):
                piece = coarse[group, q * prow : (q + 1) * prow, :]
                piece = rolled(piece, unit * q - source)
                packed = piece if packed is None else jnp.where(slot == q, piece, packed)
            sendbuf[step, group, way, side] = packed

    def convolve(step, group, way, q, weights):
        at, by = index[way], stride[way]
        count = packs * 2
        x = coarse[group, q * prow : (q + 1) * prow, :]
        before = rolled(halo[step, group, way, 0], -2 * by * q)
        after = rolled(halo[step, group, way, 1], (count - 2) * by - 2 * by * q)
        taps = (
            jnp.where(at < 2, before, rolled(x, 2 * by)),
            jnp.where(at < 1, rolled(before, -by), rolled(x, by)),
            x,
            jnp.where(at >= count - 1, rolled(after, by), rolled(x, -by)),
            jnp.where(at >= count - 2, after, rolled(x, -2 * by)),
        )
        total = None
        for d in range(5):
            k = weights[d, group * GROUP_LEVELS : (group + 1) * GROUP_LEVELS, :]
            k = jnp.concatenate([k] * (prow // GROUP_LEVELS), axis=0)
            total = k * taps[d] if total is None else total + k * taps[d]
        return total

    def project(step, group):
        for o in range(owners):
            owner = group * owners + o

            @pl.when(owner != me)
            def _():
                gathered_from(step, owner).wait_recv()

            for v in range(nvar):
                gfull[v, o * own_levels : (o + 1) * own_levels, :] = gbuf[step, owner, v]

        def one(j, carry):
            at = pl.ds(pl.multiple_of(j * LANES, LANES), LANES)
            g = [gfull[v, :, at] for v in range(nvar)]
            for k in range(members):
                total = None
                for v in range(nvar):
                    term = pert[k, v, group * GROUP_LEVELS : (group + 1) * GROUP_LEVELS, at].astype(F32) * g[v]
                    total = term if total is None else total + term
                high, low = split(total)
                alpha_hi[k * GROUP_LEVELS : (k + 1) * GROUP_LEVELS, at] = high
                alpha_lo[k * GROUP_LEVELS : (k + 1) * GROUP_LEVELS, at] = low
            return carry

        lax.fori_loop(0, cols // LANES, one, 0)
        coarse[group] = jnp.dot(
            alpha_hi[...], down_ref[...], preferred_element_type=F32
        ) + jnp.dot(alpha_lo[...], down_ref[...], preferred_element_type=F32)
        pack(step, group, 0)

        @pl.when(has_next)
        def _():
            halo_copy(step, group, 0, 0).start()

        @pl.when(has_prev)
        def _():
            halo_copy(step, group, 0, 1).start()

    def smooth_y(step, group):
        @pl.when(has_prev)
        def _():
            halo_copy(step, group, 0, 0).wait_recv()

        @pl.when(has_next)
        def _():
            halo_copy(step, group, 0, 1).wait_recv()

        for q in range(packs):
            done = convolve(step, group, 0, q, kyb)
            coarse[group, q * prow : (q + 1) * prow, :] = done
        pack(step, group, 1)
        halo_copy(step, group, 1, 0).start()
        halo_copy(step, group, 1, 1).start()

    def expand(step, group):
        halo_copy(step, group, 1, 0).wait_recv()
        halo_copy(step, group, 1, 1).wait_recv()
        each = prow // GROUP_LEVELS
        for q in range(packs):
            done = convolve(step, group, 1, q, kxb)
            factor = jnp.concatenate(
                [
                    jnp.full((GROUP_LEVELS, COARSE), weight_ref[q * each + m] * (1.0 / (n_mem * members)), F32)
                    for m in range(each)
                ],
                axis=0,
            )
            high, low = split(done * factor)
            smooth[q * prow : (q + 1) * prow, :COARSE] = high
            smooth[q * prow : (q + 1) * prow, COARSE:] = low
        fine[...] = jnp.dot(smooth[...], up_ref[...], preferred_element_type=F32)

        def one(j, carry):
            at = pl.ds(pl.multiple_of(j * LANES, LANES), LANES)
            total = [None] * nvar
            for k in range(members):
                f = fine[k * GROUP_LEVELS : (k + 1) * GROUP_LEVELS, at]
                for v in range(nvar):
                    term = pert[k, v, group * GROUP_LEVELS : (group + 1) * GROUP_LEVELS, at].astype(F32) * f
                    total[v] = term if total[v] is None else total[v] + term
            for o in range(owners):
                for v in range(nvar):
                    part[step, group * owners + o, v, :, at] = total[v][o * own_levels : (o + 1) * own_levels]
            return carry

        lax.fori_loop(0, cols // LANES, one, 0)
        for o in range(owners):
            owner = group * owners + o

            @pl.when(owner != me)
            def _():
                reduce_to(step, owner).start()

    def update(step, group):
        @pl.when(me // owners == group)
        def _():
            total = static_ref[...] * gbuf[step, me] + part[step, me]
            for i in range(1, n_mem):
                source = lax.rem(me + i, n_mem)
                reduced_from(step, source).wait_recv()
                total = total + rsbuf[step, source]
            now = ana[...]
            now = now - 0.5 * (now + total)
            if step == STEPS - 1:
                out_ref[...] = now
            else:
                ana[...] = now
                gbuf[step + 1, me] = obs[...] * (now - innov_ref[...])
                for i in range(1, n_mem):
                    gather_to(step + 1, i).start()

    for load in loads[5:]:
        load.wait()
    stages = (project, smooth_y, expand, update)
    order = [
        (PERIOD * step + DUE[i] + (1.0 if step == 0 and i < 2 else PACE) * group, group, step, i)
        for step in range(STEPS) for i in range(len(stages)) for group in range(n_group)
    ]
    for _, group, step, i in sorted(order):
        stages[i](step, group)

    for step in range(STEPS):
        for i in range(1, n_mem):
            gather_to(step, i).wait_send()
        for owner in range(n_mem):

            @pl.when(owner != me)
            def _():
                reduce_to(step, owner).wait_send()

        for group in range(n_group):

            @pl.when(has_next)
            def _():
                halo_copy(step, group, 0, 0).wait_send()

            @pl.when(has_prev)
            def _():
                halo_copy(step, group, 0, 1).wait_send()

            halo_copy(step, group, 1, 0).wait_send()
            halo_copy(step, group, 1, 1).wait_send()


def body(n_mem, n_tile, perturbations, member_weight, innovation, obs_weight, static_var, obs_mask, kernel_x, kernel_y):
    members, nvar, levels, cols = perturbations.shape
    own = innovation.shape[1]
    n_group = levels // GROUP_LEVELS
    rows = members * GROUP_LEVELS
    prow = rows // (COARSE_X // 2)
    down = interp_matrix()
    down_b = jnp.asarray(down, BF16)
    up_b = jnp.asarray(np.concatenate([down.T, down.T], axis=0), BF16)
    dma = pltpu.SemaphoreType.DMA
    return pl.pallas_call(
        functools.partial(kernel, n_mem, n_tile),
        out_shape=jax.ShapeDtypeStruct(innovation.shape, F32),
        in_specs=[pl.BlockSpec(memory_space=pl.ANY)] * 10,
        out_specs=pl.BlockSpec(memory_space=pltpu.VMEM),
        scratch_shapes=[
            pltpu.SMEM(member_weight.shape, F32),
            pltpu.VMEM(innovation.shape, F32),
            pltpu.SMEM(obs_weight.shape, F32),
            pltpu.VMEM(innovation.shape, F32),
            pltpu.VMEM((1, cols), jnp.int32),
            pltpu.VMEM((5, levels), F32),
            pltpu.VMEM((5, levels), F32),
            pltpu.VMEM(down_b.shape, BF16),
            pltpu.VMEM(up_b.shape, BF16),
            pltpu.VMEM(perturbations.shape, BF16),
            pltpu.VMEM(innovation.shape, F32),
            pltpu.VMEM(innovation.shape, F32),
            pltpu.VMEM((STEPS, n_mem) + innovation.shape, F32),
            pltpu.VMEM((STEPS, n_mem) + innovation.shape, F32),
            pltpu.VMEM((STEPS, n_mem) + innovation.shape, F32),
            pltpu.VMEM((nvar, GROUP_LEVELS, cols), F32),
            pltpu.VMEM((rows, cols), BF16),
            pltpu.VMEM((rows, cols), BF16),
            pltpu.VMEM((n_group, rows, COARSE), F32),
            pltpu.VMEM((rows, 2 * COARSE), BF16),
            pltpu.VMEM((rows, cols), F32),
            pltpu.VMEM((5, levels, COARSE), F32),
            pltpu.VMEM((5, levels, COARSE), F32),
            pltpu.VMEM((STEPS, n_group, 2, 2, prow, COARSE), F32),
            pltpu.VMEM((STEPS, n_group, 2, 2, prow, COARSE), F32),
            dma((10,)),
            dma((STEPS, n_mem)),
            dma((STEPS, n_mem)),
            dma((STEPS, n_mem)),
            dma((STEPS, n_mem)),
            dma((STEPS, n_group, 2, 2)),
            dma((STEPS, n_group, 2, 2)),
        ],
        compiler_params=pltpu.CompilerParams(
            collective_id=0, has_side_effects=True
        ),
    )(
        perturbations, member_weight, innovation, obs_weight, static_var,
        obs_mask.reshape(1, cols), kernel_x.T, kernel_y.T, down_b, up_b,
    )


def solution(mesh):
    placed = (
        P("mem", None, None, "tile"),
        P("mem"),
        P(None, "mem", "tile"),
        P(None, "mem"),
        P(None, "mem", "tile"),
        P("tile"),
        P(),
        P(),
    )
    return jax.shard_map(
        functools.partial(body, mesh.shape["mem"], mesh.shape["tile"]),
        mesh=mesh, in_specs=placed, out_specs=P(None, "mem", "tile"), check_vma=False,
    )
```

```python
import functools

import jax
import jax.numpy as jnp
import numpy as np
from jax import lax
from jax.experimental import pallas as pl
from jax.experimental.pallas import tpu as pltpu
from jax.sharding import PartitionSpec as P

TILE_X = 32
TILE_Y = 32
GRID_Y = 4
STEPS = 2
COARSE_X = TILE_X // 2
COARSE_Y = TILE_Y // 2
COARSE = COARSE_X * COARSE_Y
GROUP_LEVELS = 8
DUE = (0.0, 2.4, 5.0, 8.0)
PERIOD = 11.0
PACE = 2.1
LANES = 256
MESH = pl.DeviceIdType.MESH
F32 = jnp.float32
BF16 = jnp.bfloat16


def interp_rows(fine_count):
    coarse_count = fine_count // 2
    rows = np.zeros((fine_count, coarse_count), np.float32)
    for i in range(fine_count):
        low = min(max((i - 1) // 2, 0), coarse_count - 1)
        high = min(max((i - 1) // 2 + 1, 0), coarse_count - 1)
        fraction = 0.75 if i % 2 == 0 else 0.25
        rows[i, low] += 1.0 - fraction
        rows[i, high] += fraction
    return rows


def interp_matrix():
    rows_x, rows_y = interp_rows(TILE_X), interp_rows(TILE_Y)
    whole = rows_x[:, None, None, :] * rows_y[None, :, :, None]
    return whole.reshape(TILE_X * TILE_Y, COARSE)


def rolled(x, by):
    by = by % x.shape[1]
    return x if by == 0 else pltpu.roll(x, by, 1)


def split(x):
    high = x.astype(BF16)
    return high, (x - high.astype(F32)).astype(BF16)


def kernel(
    n_mem, n_tile,
    pert_hbm, weight_hbm, innov_hbm, obsw_hbm, static_hbm, mask_hbm, kx_hbm, ky_hbm, down_hbm, up_hbm,
    out_ref,
    weight_ref, innov_ref, obsw_ref, static_ref, mask_ref, kx_ref, ky_ref, down_ref, up_ref,
    pert, obs, fields, ana, gbuf, part, rsbuf, gcols, pcols, rscols, gfull, alpha_hi, alpha_lo, coarse, smooth, fine,
    kxb, kyb, sendbuf, halo,
    load_sem, field_send, field_recv, ag_send, ag_recv, rs_send, rs_recv, agc_send, agc_recv, rsc_send, rsc_recv, halo_send, halo_recv,
):
    members, nvar, levels, cols = pert.shape
    own_levels = innov_ref.shape[1]
    n_group = levels // GROUP_LEVELS
    owners = GROUP_LEVELS // own_levels
    rows = members * GROUP_LEVELS
    packs = COARSE_X // 2
    prow = rows // packs
    grid_x = n_tile // GRID_Y
    blocks = min(n_mem, cols // 128)
    width = cols // blocks
    me = lax.axis_index("mem")
    tile = lax.axis_index("tile")
    place_y = lax.rem(tile, GRID_Y)
    next_x = lax.rem(tile + GRID_Y, n_tile)
    prev_x = lax.rem(tile + n_tile - GRID_Y, n_tile)
    has_prev = place_y > 0
    has_next = place_y < GRID_Y - 1

    pairs = (
        (innov_hbm, innov_ref), (mask_hbm, mask_ref), (obsw_hbm, obsw_ref),
        (kx_hbm, kx_ref), (ky_hbm, ky_ref), (pert_hbm, pert), (down_hbm, down_ref),
        (weight_hbm, weight_ref), (static_hbm, static_ref), (up_hbm, up_ref),
    )
    loads = [pltpu.make_async_copy(a, b, load_sem.at[i]) for i, (a, b) in enumerate(pairs)]
    for load in loads:
        load.start()

    barrier = pltpu.get_barrier_semaphore()

    def greet(device_id):
        pl.semaphore_signal(barrier, inc=1, device_id=device_id, device_id_type=MESH)

    for i in range(1, n_mem):
        greet((lax.rem(me + i, n_mem), tile))
    greet((me, next_x))
    if grid_x > 2:
        greet((me, prev_x))

    greet((me, tile - place_y + lax.rem(place_y + GRID_Y - 1, GRID_Y)))
    greet((me, tile - place_y + lax.rem(place_y + 1, GRID_Y)))

    for load in loads[:3]:
        load.wait()
    mask = mask_ref[...].astype(F32)
    for v in range(nvar):
        for l in range(own_levels):
            obs[v, l : l + 1, :] = mask * obsw_ref[v, l]
    gbuf[me] = obs[...] * (0.0 - innov_ref[...])

    pl.semaphore_wait(barrier, n_mem - 1 + min(grid_x - 1, 2) + 2)

    def columns(block):
        return pl.ds(pl.multiple_of(block * width, 128), width)

    def remote(source, target, send, receive, member):
        return pltpu.make_async_remote_copy(
            src_ref=source, dst_ref=target, send_sem=send, recv_sem=receive,
            device_id=(member, tile), device_id_type=MESH,
        )

    def other(i):
        return lax.rem(me + i, n_mem)

    def each_block(do, mine=False):
        for i in range(0 if mine else 1, n_mem):
            if blocks == n_mem:
                do(other(i))
            else:
                pl.when(other(i) < blocks)(functools.partial(do, other(i)))

    def if_block(do):
        if blocks == n_mem:
            do()
        else:
            pl.when(me < blocks)(do)

    def gather(owner, to):
        return remote(gbuf.at[owner], gbuf.at[owner], ag_send.at[to], ag_recv.at[owner], to)

    def field(f, owner, to):
        source = (static_ref, obs)[f]
        return remote(
            source.at[:, :, columns(to)], fields.at[f, owner],
            field_send.at[f, to], field_recv.at[f, owner], to,
        )

    def reduce_columns(group, source, to):
        return remote(
            pcols.at[group, to], rscols.at[group, source],
            rsc_send.at[group, to], rsc_recv.at[group, source], to,
        )

    def gather_columns(group, block, to):
        return remote(
            gcols.at[group, block], gcols.at[group, block],
            agc_send.at[group, to], agc_recv.at[group, block], to,
        )

    def reduce_levels(source, to):
        return remote(part.at[to], rsbuf.at[source], rs_send.at[to], rs_recv.at[source], to)

    def halo_copy(step, group, way, side):
        target = ((tile + 1, tile - 1), (next_x, prev_x))[way][side]
        return pltpu.make_async_remote_copy(
            src_ref=sendbuf.at[step, group, way, side], dst_ref=halo.at[step, group, way, side],
            send_sem=halo_send.at[step, group, way, side],
            recv_sem=halo_recv.at[step, group, way, side],
            device_id=(me, target), device_id_type=MESH,
        )

    for i in range(1, n_mem):
        gather(me, other(i)).start()
    loads[8].wait()

    def send_fields(to):
        for f in range(2):
            field(f, me, to).start()

    each_block(send_fields)

    def keep_fields():
        fields[0, me] = static_ref[:, :, columns(me)]
        fields[1, me] = obs[:, :, columns(me)]

    if_block(keep_fields)

    for load in loads[3:5]:
        load.wait()
    shape = (levels, levels)
    diagonal = lax.broadcasted_iota(jnp.int32, shape, 0) == lax.broadcasted_iota(jnp.int32, shape, 1)
    for source, spread in ((kx_ref, kxb), (ky_ref, kyb)):
        for d in range(5):
            column = jnp.where(diagonal, jnp.broadcast_to(source[d : d + 1, :], shape), 0.0)
            spread[d] = jnp.broadcast_to(jnp.sum(column, axis=1, keepdims=True), (levels, COARSE))

    @pl.when(jnp.logical_not(has_prev))
    def _():
        for step in range(STEPS):
            for group in range(n_group):
                halo[step, group, 0, 0] = jnp.zeros((prow, COARSE), F32)

    @pl.when(jnp.logical_not(has_next))
    def _():
        for step in range(STEPS):
            for group in range(n_group):
                halo[step, group, 0, 1] = jnp.zeros((prow, COARSE), F32)

    lane = lax.broadcasted_iota(jnp.int32, (prow, COARSE), 1)
    index = (lane // COARSE_X, lane % COARSE_X)
    stride = (COARSE_X, 1)

    def pack(step, group, way):
        slot = index[way] // 2
        unit = 2 * stride[way]
        for side, source in ((0, (packs * 2 - 2) * stride[way]), (1, 0)):
            packed = None
            for q in range(packs):
                piece = coarse[group, q * prow : (q + 1) * prow, :]
                piece = rolled(piece, unit * q - source)
                packed = piece if packed is None else jnp.where(slot == q, piece, packed)
            sendbuf[step, group, way, side] = packed

    def convolve(step, group, way, q, weights):
        at, by = index[way], stride[way]
        count = packs * 2
        x = coarse[group, q * prow : (q + 1) * prow, :]
        before = rolled(halo[step, group, way, 0], -2 * by * q)
        after = rolled(halo[step, group, way, 1], (count - 2) * by - 2 * by * q)
        taps = (
            jnp.where(at < 2, before, rolled(x, 2 * by)),
            jnp.where(at < 1, rolled(before, -by), rolled(x, by)),
            x,
            jnp.where(at >= count - 1, rolled(after, by), rolled(x, -by)),
            jnp.where(at >= count - 2, after, rolled(x, -2 * by)),
        )
        total = None
        for d in range(5):
            k = weights[d, group * GROUP_LEVELS : (group + 1) * GROUP_LEVELS, :]
            k = jnp.concatenate([k] * (prow // GROUP_LEVELS), axis=0)
            total = k * taps[d] if total is None else total + k * taps[d]
        return total

    def of_group(f, group, v):
        return jnp.concatenate([fields[f, group * owners + o, v] for o in range(owners)], axis=0)

    def project(step, group):
        if step == 0:
            for o in range(owners):
                owner = group * owners + o

                @pl.when(owner != me)
                def _():
                    gather(owner, owner).wait_recv()

                for v in range(nvar):
                    gfull[group, v, o * own_levels : (o + 1) * own_levels, :] = gbuf[owner, v]
        else:
            each_block(lambda block: gather_columns(group, block, block).wait_recv())
            for block in range(blocks):
                gfull[group, :, :, block * width : (block + 1) * width] = gcols[group, block]

        def one(j, carry):
            at = pl.ds(pl.multiple_of(j * LANES, LANES), LANES)
            g = [gfull[group, v, :, at] for v in range(nvar)]
            for k in range(members):
                total = None
                for v in range(nvar):
                    term = pert[k, v, group * GROUP_LEVELS : (group + 1) * GROUP_LEVELS, at].astype(F32) * g[v]
                    total = term if total is None else total + term
                high, low = split(total)
                alpha_hi[k * GROUP_LEVELS : (k + 1) * GROUP_LEVELS, at] = high
                alpha_lo[k * GROUP_LEVELS : (k + 1) * GROUP_LEVELS, at] = low
            return carry

        lax.fori_loop(0, cols // LANES, one, 0)
        coarse[group] = jnp.dot(
            alpha_hi[...], down_ref[...], preferred_element_type=F32
        ) + jnp.dot(alpha_lo[...], down_ref[...], preferred_element_type=F32)
        pack(step, group, 0)

        @pl.when(has_next)
        def _():
            halo_copy(step, group, 0, 0).start()

        @pl.when(has_prev)
        def _():
            halo_copy(step, group, 0, 1).start()

    def smooth_y(step, group):
        @pl.when(has_prev)
        def _():
            halo_copy(step, group, 0, 0).wait_recv()

        @pl.when(has_next)
        def _():
            halo_copy(step, group, 0, 1).wait_recv()

        for q in range(packs):
            done = convolve(step, group, 0, q, kyb)
            coarse[group, q * prow : (q + 1) * prow, :] = done
        pack(step, group, 1)
        halo_copy(step, group, 1, 0).start()
        halo_copy(step, group, 1, 1).start()

    def expand(step, group):
        halo_copy(step, group, 1, 0).wait_recv()
        halo_copy(step, group, 1, 1).wait_recv()
        each = prow // GROUP_LEVELS
        for q in range(packs):
            done = convolve(step, group, 1, q, kxb)
            factor = jnp.concatenate(
                [
                    jnp.full((GROUP_LEVELS, COARSE), weight_ref[q * each + m] * (1.0 / (n_mem * members)), F32)
                    for m in range(each)
                ],
                axis=0,
            )
            high, low = split(done * factor)
            smooth[q * prow : (q + 1) * prow, :COARSE] = high
            smooth[q * prow : (q + 1) * prow, COARSE:] = low
        fine[...] = jnp.dot(smooth[...], up_ref[...], preferred_element_type=F32)

        def one(j, carry):
            at = pl.ds(pl.multiple_of(j * LANES, LANES), LANES)
            total = [None] * nvar
            for k in range(members):
                f = fine[k * GROUP_LEVELS : (k + 1) * GROUP_LEVELS, at]
                for v in range(nvar):
                    term = pert[k, v, group * GROUP_LEVELS : (group + 1) * GROUP_LEVELS, at].astype(F32) * f
                    total[v] = term if total[v] is None else total[v] + term
            if step == 0:
                for v in range(nvar):
                    for b in range(LANES // chunk):
                        piece = total[v][:, b * chunk : (b + 1) * chunk]
                        block = j * LANES // width if chunk == LANES else j * (LANES // chunk) + b
                        inside = j * LANES % width if chunk == LANES else 0
                        pcols[group, block, v, :, pl.ds(pl.multiple_of(inside, 128), chunk)] = piece
            else:
                for o in range(owners):
                    for v in range(nvar):
                        part[group * owners + o, v, :, at] = total[v][o * own_levels : (o + 1) * own_levels]
            return carry

        chunk = min(LANES, width)
        lax.fori_loop(0, cols // LANES, one, 0)
        if step == 0:
            each_block(lambda block: reduce_columns(group, me, block).start())
            return

        def add_rest():
            for v in range(nvar):
                rest = of_group(0, group, v) * gcols[group, me, v] - ana[group, v]
                for o in range(owners):
                    part[group * owners + o, v, :, columns(me)] += rest[o * own_levels : (o + 1) * own_levels]

        if_block(add_rest)
        for o in range(owners):
            owner = group * owners + o

            @pl.when(owner != me)
            def _():
                reduce_levels(me, owner).start()

    def update(step, group):
        if step == 0:
            def by_columns():
                for o in range(owners):
                    owner = group * owners + o

                    @pl.when(owner != me)
                    def _():
                        field(0, owner, owner).wait_recv()
                        field(1, owner, owner).wait_recv()

                for i in range(1, n_mem):
                    reduce_columns(group, other(i), other(i)).wait_recv()
                for v in range(nvar):
                    before = gfull[group, v, :, columns(me)]
                    total = of_group(0, group, v) * before + pcols[group, me, v]
                    for i in range(1, n_mem):
                        total = total + rscols[group, other(i), v]
                    now = -0.5 * total
                    ana[group, v] = now
                    gcols[group, me, v] = of_group(1, group, v) * now + before
                for i in range(1, n_mem):
                    gather_columns(group, me, other(i)).start()

            if_block(by_columns)
        else:

            @pl.when(me // owners == group)
            def _():
                total = part[me]
                for i in range(1, n_mem):
                    reduce_levels(other(i), other(i)).wait_recv()
                    total = total + rsbuf[other(i)]
                out_ref[...] = -0.5 * total

    for load in loads[5:8] + loads[9:]:
        load.wait()
    stages = (project, smooth_y, expand, update)
    order = [
        (PERIOD * step + DUE[i] + (1.0 if step == 0 and i < 2 else PACE) * group + 4.0 * (step * i // 3), group, step, i)
        for step in range(STEPS) for i in range(len(stages)) for group in range(n_group)
    ]
    for _, group, step, i in sorted(order):
        stages[i](step, group)

    for i in range(1, n_mem):
        gather(me, other(i)).wait_send()
        reduce_levels(me, other(i)).wait_send()

    def sent(to):
        for f in range(2):
            field(f, me, to).wait_send()
        for group in range(n_group):
            reduce_columns(group, me, to).wait_send()

    each_block(sent)

    def sent_columns():
        for i in range(1, n_mem):
            for group in range(n_group):
                gather_columns(group, me, other(i)).wait_send()

    if_block(sent_columns)
    for step in range(STEPS):
        for group in range(n_group):

            @pl.when(has_next)
            def _():
                halo_copy(step, group, 0, 0).wait_send()

            @pl.when(has_prev)
            def _():
                halo_copy(step, group, 0, 1).wait_send()

            halo_copy(step, group, 1, 0).wait_send()
            halo_copy(step, group, 1, 1).wait_send()


def body(n_mem, n_tile, perturbations, member_weight, innovation, obs_weight, static_var, obs_mask, kernel_x, kernel_y):
    members, nvar, levels, cols = perturbations.shape
    own = innovation.shape[1]
    n_group = levels // GROUP_LEVELS
    rows = members * GROUP_LEVELS
    prow = rows // (COARSE_X // 2)
    blocks = min(n_mem, cols // 128)
    width = cols // blocks
    down = interp_matrix()
    down_b = jnp.asarray(down, BF16)
    up_b = jnp.asarray(np.concatenate([down.T, down.T], axis=0), BF16)
    dma = pltpu.SemaphoreType.DMA
    return pl.pallas_call(
        functools.partial(kernel, n_mem, n_tile),
        out_shape=jax.ShapeDtypeStruct(innovation.shape, F32),
        in_specs=[pl.BlockSpec(memory_space=pl.ANY)] * 10,
        out_specs=pl.BlockSpec(memory_space=pltpu.VMEM),
        scratch_shapes=[
            pltpu.SMEM(member_weight.shape, F32),
            pltpu.VMEM(innovation.shape, F32),
            pltpu.SMEM(obs_weight.shape, F32),
            pltpu.VMEM(innovation.shape, F32),
            pltpu.VMEM((1, cols), jnp.int32),
            pltpu.VMEM((5, levels), F32),
            pltpu.VMEM((5, levels), F32),
            pltpu.VMEM(down_b.shape, BF16),
            pltpu.VMEM(up_b.shape, BF16),
            pltpu.VMEM(perturbations.shape, BF16),
            pltpu.VMEM(innovation.shape, F32),
            pltpu.VMEM((2, n_mem, nvar, own, width), F32),
            pltpu.VMEM((n_group, nvar, GROUP_LEVELS, width), F32),
            pltpu.VMEM((n_mem,) + innovation.shape, F32),
            pltpu.VMEM((n_mem,) + innovation.shape, F32),
            pltpu.VMEM((n_mem,) + innovation.shape, F32),
            pltpu.VMEM((n_group, blocks, nvar, GROUP_LEVELS, width), F32),
            pltpu.VMEM((n_group, blocks, nvar, GROUP_LEVELS, width), F32),
            pltpu.VMEM((n_group, n_mem, nvar, GROUP_LEVELS, width), F32),
            pltpu.VMEM((n_group, nvar, GROUP_LEVELS, cols), F32),
            pltpu.VMEM((rows, cols), BF16),
            pltpu.VMEM((rows, cols), BF16),
            pltpu.VMEM((n_group, rows, COARSE), F32),
            pltpu.VMEM((rows, 2 * COARSE), BF16),
            pltpu.VMEM((rows, cols), F32),
            pltpu.VMEM((5, levels, COARSE), F32),
            pltpu.VMEM((5, levels, COARSE), F32),
            pltpu.VMEM((STEPS, n_group, 2, 2, prow, COARSE), F32),
            pltpu.VMEM((STEPS, n_group, 2, 2, prow, COARSE), F32),
            dma((10,)),
            dma((2, n_mem)),
            dma((2, n_mem)),
            dma((n_mem,)),
            dma((n_mem,)),
            dma((n_mem,)),
            dma((n_mem,)),
            dma((n_group, n_mem)),
            dma((n_group, n_mem)),
            dma((n_group, n_mem)),
            dma((n_group, n_mem)),
            dma((STEPS, n_group, 2, 2)),
            dma((STEPS, n_group, 2, 2)),
        ],
        compiler_params=pltpu.CompilerParams(
            collective_id=0, has_side_effects=True
        ),
    )(
        perturbations, member_weight, innovation, obs_weight, static_var,
        obs_mask.reshape(1, cols), kernel_x.T, kernel_y.T, down_b, up_b,
    )


def solution(mesh):
    placed = (
        P("mem", None, None, "tile"),
        P("mem"),
        P(None, "mem", "tile"),
        P(None, "mem"),
        P(None, "mem", "tile"),
        P("tile"),
        P(),
        P(),
    )
    return jax.shard_map(
        functools.partial(body, mesh.shape["mem"], mesh.shape["tile"]),
        mesh=mesh, in_specs=placed, out_specs=P(None, "mem", "tile"), check_vma=False,
    )
```

```python
import functools

import jax
import jax.numpy as jnp
import numpy as np
from jax import lax
from jax.experimental import pallas as pl
from jax.experimental.pallas import tpu as pltpu
from jax.sharding import PartitionSpec as P

TILE_X = 32
TILE_Y = 32
GRID_Y = 4
STEPS = 2
COARSE_X = TILE_X // 2
COARSE_Y = TILE_Y // 2
COARSE = COARSE_X * COARSE_Y
GROUP_LEVELS = 8
DUE = (0.0, 100.0, 200.0, 300.0)
PERIOD = 1000.0
PACE = 2.1
LANES = 256
MESH = pl.DeviceIdType.MESH
F32 = jnp.float32
BF16 = jnp.bfloat16


def interp_rows(fine_count):
    coarse_count = fine_count // 2
    rows = np.zeros((fine_count, coarse_count), np.float32)
    for i in range(fine_count):
        low = min(max((i - 1) // 2, 0), coarse_count - 1)
        high = min(max((i - 1) // 2 + 1, 0), coarse_count - 1)
        fraction = 0.75 if i % 2 == 0 else 0.25
        rows[i, low] += 1.0 - fraction
        rows[i, high] += fraction
    return rows


def interp_matrix():
    rows_x, rows_y = interp_rows(TILE_X), interp_rows(TILE_Y)
    whole = rows_x[:, None, None, :] * rows_y[None, :, :, None]
    return whole.reshape(TILE_X * TILE_Y, COARSE)


def rolled(x, by):
    by = by % x.shape[1]
    return x if by == 0 else pltpu.roll(x, by, 1)


def split(x):
    high = x.astype(BF16)
    return high, (x - high.astype(F32)).astype(BF16)


def kernel(
    n_mem, n_tile,
    pert_hbm, weight_hbm, innov_hbm, obsw_hbm, static_hbm, mask_hbm, kx_hbm, ky_hbm, down_hbm, up_hbm,
    out_ref,
    weight_ref, innov_ref, obsw_ref, static_ref, mask_ref, kx_ref, ky_ref, down_ref, up_ref,
    pert, obs, fields, ana, gbuf, part, rsbuf, gcols, pcols, rscols, gfull, alpha_hi, alpha_lo, coarse, smooth, fine,
    kxb, kyb, sendbuf, halo,
    load_sem, field_send, field_recv, ag_send, ag_recv, rs_send, rs_recv, agc_send, agc_recv, rsc_send, rsc_recv, halo_send, halo_recv,
):
    members, nvar, levels, cols = pert.shape
    own_levels = innov_ref.shape[1]
    n_group = levels // GROUP_LEVELS
    owners = GROUP_LEVELS // own_levels
    rows = members * GROUP_LEVELS
    packs = COARSE_X // 2
    prow = rows // packs
    grid_x = n_tile // GRID_Y
    blocks = min(n_mem, cols // 128)
    width = cols // blocks
    me = lax.axis_index("mem")
    tile = lax.axis_index("tile")
    place_y = lax.rem(tile, GRID_Y)
    next_x = lax.rem(tile + GRID_Y, n_tile)
    prev_x = lax.rem(tile + n_tile - GRID_Y, n_tile)
    has_prev = place_y > 0
    has_next = place_y < GRID_Y - 1

    pairs = (
        (innov_hbm, innov_ref), (mask_hbm, mask_ref), (obsw_hbm, obsw_ref),
        (kx_hbm, kx_ref), (ky_hbm, ky_ref), (pert_hbm, pert), (down_hbm, down_ref),
        (weight_hbm, weight_ref), (static_hbm, static_ref), (up_hbm, up_ref),
    )
    loads = [pltpu.make_async_copy(a, b, load_sem.at[i]) for i, (a, b) in enumerate(pairs)]
    for load in loads:
        load.start()

    barrier = pltpu.get_barrier_semaphore()

    def greet(device_id):
        pl.semaphore_signal(barrier, inc=1, device_id=device_id, device_id_type=MESH)

    for i in range(1, n_mem):
        greet((lax.rem(me + i, n_mem), tile))
    greet((me, next_x))
    if grid_x > 2:
        greet((me, prev_x))

    greet((me, tile - place_y + lax.rem(place_y + GRID_Y - 1, GRID_Y)))
    greet((me, tile - place_y + lax.rem(place_y + 1, GRID_Y)))

    for load in loads[:3]:
        load.wait()
    mask = mask_ref[...].astype(F32)
    for v in range(nvar):
        for l in range(own_levels):
            obs[v, l : l + 1, :] = mask * obsw_ref[v, l]
    gbuf[me] = obs[...] * (0.0 - innov_ref[...])

    pl.semaphore_wait(barrier, n_mem - 1 + min(grid_x - 1, 2) + 2)

    def columns(block):
        return pl.ds(pl.multiple_of(block * width, 128), width)

    def remote(source, target, send, receive, member):
        return pltpu.make_async_remote_copy(
            src_ref=source, dst_ref=target, send_sem=send, recv_sem=receive,
            device_id=(member, tile), device_id_type=MESH,
        )

    def other(i):
        return lax.rem(me + i, n_mem)

    def each_block(do, mine=False):
        for i in range(0 if mine else 1, n_mem):
            if blocks == n_mem:
                do(other(i))
            else:
                pl.when(other(i) < blocks)(functools.partial(do, other(i)))

    def if_block(do):
        if blocks == n_mem:
            do()
        else:
            pl.when(me < blocks)(do)

    def gather(owner, to):
        return remote(gbuf.at[owner], gbuf.at[owner], ag_send.at[to], ag_recv.at[owner], to)

    def field(f, owner, to):
        source = (static_ref, obs)[f]
        return remote(
            source.at[:, :, columns(to)], fields.at[f, owner],
            field_send.at[f, to], field_recv.at[f, owner], to,
        )

    def reduce_columns(group, source, to):
        return remote(
            pcols.at[group, to], rscols.at[group, source],
            rsc_send.at[group, to], rsc_recv.at[group, source], to,
        )

    def gather_columns(group, block, to):
        return remote(
            gcols.at[group, block], gcols.at[group, block],
            agc_send.at[group, to], agc_recv.at[group, block], to,
        )

    def reduce_levels(source, to):
        return remote(part.at[to], rsbuf.at[source], rs_send.at[to], rs_recv.at[source], to)

    def halo_copy(step, group, way, side):
        target = ((tile + 1, tile - 1), (next_x, prev_x))[way][side]
        return pltpu.make_async_remote_copy(
            src_ref=sendbuf.at[step, group, way, side], dst_ref=halo.at[step, group, way, side],
            send_sem=halo_send.at[step, group, way, side],
            recv_sem=halo_recv.at[step, group, way, side],
            device_id=(me, target), device_id_type=MESH,
        )

    for i in range(1, n_mem):
        gather(me, other(i)).start()
    loads[8].wait()

    def send_fields(to):
        for f in range(2):
            field(f, me, to).start()

    each_block(send_fields)

    def keep_fields():
        fields[0, me] = static_ref[:, :, columns(me)]
        fields[1, me] = obs[:, :, columns(me)]

    if_block(keep_fields)

    for load in loads[3:5]:
        load.wait()
    shape = (levels, levels)
    diagonal = lax.broadcasted_iota(jnp.int32, shape, 0) == lax.broadcasted_iota(jnp.int32, shape, 1)
    for source, spread in ((kx_ref, kxb), (ky_ref, kyb)):
        for d in range(5):
            column = jnp.where(diagonal, jnp.broadcast_to(source[d : d + 1, :], shape), 0.0)
            spread[d] = jnp.broadcast_to(jnp.sum(column, axis=1, keepdims=True), (levels, COARSE))

    @pl.when(jnp.logical_not(has_prev))
    def _():
        for step in range(STEPS):
            for group in range(n_group):
                halo[step, group, 0, 0] = jnp.zeros((prow, COARSE), F32)

    @pl.when(jnp.logical_not(has_next))
    def _():
        for step in range(STEPS):
            for group in range(n_group):
                halo[step, group, 0, 1] = jnp.zeros((prow, COARSE), F32)

    lane = lax.broadcasted_iota(jnp.int32, (prow, COARSE), 1)
    index = (lane // COARSE_X, lane % COARSE_X)
    stride = (COARSE_X, 1)

    def pack(step, group, way):
        slot = index[way] // 2
        unit = 2 * stride[way]
        for side, source in ((0, (packs * 2 - 2) * stride[way]), (1, 0)):
            packed = None
            for q in range(packs):
                piece = coarse[group, q * prow : (q + 1) * prow, :]
                piece = rolled(piece, unit * q - source)
                packed = piece if packed is None else jnp.where(slot == q, piece, packed)
            sendbuf[step, group, way, side] = packed

    def convolve(step, group, way, q, weights):
        at, by = index[way], stride[way]
        count = packs * 2
        x = coarse[group, q * prow : (q + 1) * prow, :]
        before = rolled(halo[step, group, way, 0], -2 * by * q)
        after = rolled(halo[step, group, way, 1], (count - 2) * by - 2 * by * q)
        taps = (
            jnp.where(at < 2, before, rolled(x, 2 * by)),
            jnp.where(at < 1, rolled(before, -by), rolled(x, by)),
            x,
            jnp.where(at >= count - 1, rolled(after, by), rolled(x, -by)),
            jnp.where(at >= count - 2, after, rolled(x, -2 * by)),
        )
        total = None
        for d in range(5):
            k = weights[d, group * GROUP_LEVELS : (group + 1) * GROUP_LEVELS, :]
            k = jnp.concatenate([k] * (prow // GROUP_LEVELS), axis=0)
            total = k * taps[d] if total is None else total + k * taps[d]
        return total

    def of_group(f, group, v):
        return jnp.concatenate([fields[f, group * owners + o, v] for o in range(owners)], axis=0)

    def project(step, group):
        if step == 0:
            for o in range(owners):
                owner = group * owners + o

                @pl.when(owner != me)
                def _():
                    gather(owner, owner).wait_recv()

                for v in range(nvar):
                    gfull[group, v, o * own_levels : (o + 1) * own_levels, :] = gbuf[owner, v]
        else:
            each_block(lambda block: gather_columns(group, block, block).wait_recv())
            for block in range(blocks):
                gfull[group, :, :, block * width : (block + 1) * width] = gcols[group, block]

        def one(j, carry):
            at = pl.ds(pl.multiple_of(j * LANES, LANES), LANES)
            g = [gfull[group, v, :, at] for v in range(nvar)]
            for k in range(members):
                total = None
                for v in range(nvar):
                    term = pert[k, v, group * GROUP_LEVELS : (group + 1) * GROUP_LEVELS, at].astype(F32) * g[v]
                    total = term if total is None else total + term
                high, low = split(total)
                alpha_hi[k * GROUP_LEVELS : (k + 1) * GROUP_LEVELS, at] = high
                alpha_lo[k * GROUP_LEVELS : (k + 1) * GROUP_LEVELS, at] = low
            return carry

        lax.fori_loop(0, cols // LANES, one, 0)
        coarse[group] = jnp.dot(
            alpha_hi[...], down_ref[...], preferred_element_type=F32
        ) + jnp.dot(alpha_lo[...], down_ref[...], preferred_element_type=F32)
        pack(step, group, 0)

        @pl.when(has_next)
        def _():
            halo_copy(step, group, 0, 0).start()

        @pl.when(has_prev)
        def _():
            halo_copy(step, group, 0, 1).start()

    def smooth_y(step, group):
        @pl.when(has_prev)
        def _():
            halo_copy(step, group, 0, 0).wait_recv()

        @pl.when(has_next)
        def _():
            halo_copy(step, group, 0, 1).wait_recv()

        for q in range(packs):
            done = convolve(step, group, 0, q, kyb)
            coarse[group, q * prow : (q + 1) * prow, :] = done
        pack(step, group, 1)
        halo_copy(step, group, 1, 0).start()
        halo_copy(step, group, 1, 1).start()

    def expand(step, group):
        halo_copy(step, group, 1, 0).wait_recv()
        halo_copy(step, group, 1, 1).wait_recv()
        each = prow // GROUP_LEVELS
        for q in range(packs):
            done = convolve(step, group, 1, q, kxb)
            factor = jnp.concatenate(
                [
                    jnp.full((GROUP_LEVELS, COARSE), weight_ref[q * each + m] * (1.0 / (n_mem * members)), F32)
                    for m in range(each)
                ],
                axis=0,
            )
            high, low = split(done * factor)
            smooth[q * prow : (q + 1) * prow, :COARSE] = high
            smooth[q * prow : (q + 1) * prow, COARSE:] = low
        fine[...] = jnp.dot(smooth[...], up_ref[...], preferred_element_type=F32)

        def one(j, carry):
            at = pl.ds(pl.multiple_of(j * LANES, LANES), LANES)
            total = [None] * nvar
            for k in range(members):
                f = fine[k * GROUP_LEVELS : (k + 1) * GROUP_LEVELS, at]
                for v in range(nvar):
                    term = pert[k, v, group * GROUP_LEVELS : (group + 1) * GROUP_LEVELS, at].astype(F32) * f
                    total[v] = term if total[v] is None else total[v] + term
            if step == 0:
                for v in range(nvar):
                    for b in range(LANES // chunk):
                        piece = total[v][:, b * chunk : (b + 1) * chunk]
                        block = j * LANES // width if chunk == LANES else j * (LANES // chunk) + b
                        inside = j * LANES % width if chunk == LANES else 0
                        pcols[group, block, v, :, pl.ds(pl.multiple_of(inside, 128), chunk)] = piece
            else:
                for o in range(owners):
                    for v in range(nvar):
                        part[group * owners + o, v, :, at] = total[v][o * own_levels : (o + 1) * own_levels]
            return carry

        chunk = min(LANES, width)
        lax.fori_loop(0, cols // LANES, one, 0)
        if step == 0:
            each_block(lambda block: reduce_columns(group, me, block).start())
            return

        def add_rest():
            for v in range(nvar):
                rest = of_group(0, group, v) * gcols[group, me, v] - ana[group, v]
                for o in range(owners):
                    part[group * owners + o, v, :, columns(me)] += rest[o * own_levels : (o + 1) * own_levels]

        if_block(add_rest)
        for o in range(owners):
            owner = group * owners + o

            @pl.when(owner != me)
            def _():
                reduce_levels(me, owner).start()

    def update(step, group):
        if step == 0:
            def by_columns():
                for o in range(owners):
                    owner = group * owners + o

                    @pl.when(owner != me)
                    def _():
                        field(0, owner, owner).wait_recv()
                        field(1, owner, owner).wait_recv()

                for i in range(1, n_mem):
                    reduce_columns(group, other(i), other(i)).wait_recv()
                for v in range(nvar):
                    before = gfull[group, v, :, columns(me)]
                    total = of_group(0, group, v) * before + pcols[group, me, v]
                    for i in range(1, n_mem):
                        total = total + rscols[group, other(i), v]
                    now = -0.5 * total
                    ana[group, v] = now
                    gcols[group, me, v] = of_group(1, group, v) * now + before
                for i in range(1, n_mem):
                    gather_columns(group, me, other(i)).start()

            if_block(by_columns)
        else:

            @pl.when(me // owners == group)
            def _():
                total = part[me]
                for i in range(1, n_mem):
                    reduce_levels(other(i), other(i)).wait_recv()
                    total = total + rsbuf[other(i)]
                out_ref[...] = -0.5 * total

    for load in loads[5:8] + loads[9:]:
        load.wait()
    stages = (project, smooth_y, expand, update)
    order = [
        (PERIOD * step + DUE[i] + (1.0 if step == 0 and i < 2 else PACE) * group + 4.0 * (step * i // 3), group, step, i)
        for step in range(STEPS) for i in range(len(stages)) for group in range(n_group)
    ]
    for _, group, step, i in sorted(order):
        stages[i](step, group)

    for i in range(1, n_mem):
        gather(me, other(i)).wait_send()
        reduce_levels(me, other(i)).wait_send()

    def sent(to):
        for f in range(2):
            field(f, me, to).wait_send()
        for group in range(n_group):
            reduce_columns(group, me, to).wait_send()

    each_block(sent)

    def sent_columns():
        for i in range(1, n_mem):
            for group in range(n_group):
                gather_columns(group, me, other(i)).wait_send()

    if_block(sent_columns)
    for step in range(STEPS):
        for group in range(n_group):

            @pl.when(has_next)
            def _():
                halo_copy(step, group, 0, 0).wait_send()

            @pl.when(has_prev)
            def _():
                halo_copy(step, group, 0, 1).wait_send()

            halo_copy(step, group, 1, 0).wait_send()
            halo_copy(step, group, 1, 1).wait_send()


def body(n_mem, n_tile, perturbations, member_weight, innovation, obs_weight, static_var, obs_mask, kernel_x, kernel_y):
    members, nvar, levels, cols = perturbations.shape
    own = innovation.shape[1]
    n_group = levels // GROUP_LEVELS
    rows = members * GROUP_LEVELS
    prow = rows // (COARSE_X // 2)
    blocks = min(n_mem, cols // 128)
    width = cols // blocks
    down = interp_matrix()
    down_b = jnp.asarray(down, BF16)
    up_b = jnp.asarray(np.concatenate([down.T, down.T], axis=0), BF16)
    dma = pltpu.SemaphoreType.DMA
    return pl.pallas_call(
        functools.partial(kernel, n_mem, n_tile),
        out_shape=jax.ShapeDtypeStruct(innovation.shape, F32),
        in_specs=[pl.BlockSpec(memory_space=pl.ANY)] * 10,
        out_specs=pl.BlockSpec(memory_space=pltpu.VMEM),
        scratch_shapes=[
            pltpu.SMEM(member_weight.shape, F32),
            pltpu.VMEM(innovation.shape, F32),
            pltpu.SMEM(obs_weight.shape, F32),
            pltpu.VMEM(innovation.shape, F32),
            pltpu.VMEM((1, cols), jnp.int32),
            pltpu.VMEM((5, levels), F32),
            pltpu.VMEM((5, levels), F32),
            pltpu.VMEM(down_b.shape, BF16),
            pltpu.VMEM(up_b.shape, BF16),
            pltpu.VMEM(perturbations.shape, BF16),
            pltpu.VMEM(innovation.shape, F32),
            pltpu.VMEM((2, n_mem, nvar, own, width), F32),
            pltpu.VMEM((n_group, nvar, GROUP_LEVELS, width), F32),
            pltpu.VMEM((n_mem,) + innovation.shape, F32),
            pltpu.VMEM((n_mem,) + innovation.shape, F32),
            pltpu.VMEM((n_mem,) + innovation.shape, F32),
            pltpu.VMEM((n_group, blocks, nvar, GROUP_LEVELS, width), F32),
            pltpu.VMEM((n_group, blocks, nvar, GROUP_LEVELS, width), F32),
            pltpu.VMEM((n_group, n_mem, nvar, GROUP_LEVELS, width), F32),
            pltpu.VMEM((n_group, nvar, GROUP_LEVELS, cols), F32),
            pltpu.VMEM((rows, cols), BF16),
            pltpu.VMEM((rows, cols), BF16),
            pltpu.VMEM((n_group, rows, COARSE), F32),
            pltpu.VMEM((rows, 2 * COARSE), BF16),
            pltpu.VMEM((rows, cols), F32),
            pltpu.VMEM((5, levels, COARSE), F32),
            pltpu.VMEM((5, levels, COARSE), F32),
            pltpu.VMEM((STEPS, n_group, 2, 2, prow, COARSE), F32),
            pltpu.VMEM((STEPS, n_group, 2, 2, prow, COARSE), F32),
            dma((10,)),
            dma((2, n_mem)),
            dma((2, n_mem)),
            dma((n_mem,)),
            dma((n_mem,)),
            dma((n_mem,)),
            dma((n_mem,)),
            dma((n_group, n_mem)),
            dma((n_group, n_mem)),
            dma((n_group, n_mem)),
            dma((n_group, n_mem)),
            dma((STEPS, n_group, 2, 2)),
            dma((STEPS, n_group, 2, 2)),
        ],
        compiler_params=pltpu.CompilerParams(
            collective_id=0, has_side_effects=True
        ),
    )(
        perturbations, member_weight, innovation, obs_weight, static_var,
        obs_mask.reshape(1, cols), kernel_x.T, kernel_y.T, down_b, up_b,
    )


def solution(mesh):
    placed = (
        P("mem", None, None, "tile"),
        P("mem"),
        P(None, "mem", "tile"),
        P(None, "mem"),
        P(None, "mem", "tile"),
        P("tile"),
        P(),
        P(),
    )
    return jax.shard_map(
        functools.partial(body, mesh.shape["mem"], mesh.shape["tile"]),
        mesh=mesh, in_specs=placed, out_specs=P(None, "mem", "tile"), check_vma=False,
    )
```
